128 devices in a mesh: ctx: 32 (over x, y, core), head: 4 (over z).
Axes of the slice: x: 4, y: 4, z: 4, core: 2. Of those that a mesh axis runs over, the one named last changes fastest.
Arguments:
- tokens: bfloat16 [8192, 2048], P(('ctx', 'head')), may hold values from -6 to 6
- w_query: bfloat16 [2048, 2048], P(None, 'head'), may hold values from -0.125 to 0.125
- w_key_first: bfloat16 [2048, 2048], P(None, 'head'), may hold values from -0.125 to 0.125
- w_key_second: bfloat16 [2048, 2048], P(None, 'head'), may hold values from -0.125 to 0.125
- w_value_first: bfloat16 [2048, 2048], P(None, 'head'), may hold values from -0.125 to 0.125
- w_value_second: bfloat16 [2048, 2048], P(None, 'head'), may hold values from -0.125 to 0.125
- w_out: bfloat16 [2048, 2048], P('head'), may hold values from -0.125 to 0.125
- lengths: int32 [16], replicated, may hold values from 1 to 4352, 8192 in all
- out_cotangent: bfloat16 [8192, 2048], P(('ctx', 'head')), may hold values from -6 to 6
Outputs:
- result: bfloat16 [8192, 2048], P(('ctx', 'head'))
- grad_tokens: bfloat16 [8192, 2048], P(('ctx', 'head'))
The draws below stay inside these ranges and needn't reach their ends.
Inputs may be any that keep to these rules, and one draw needn't show every extreme that they name: Document lengths sum to 8192; the longest holds exactly 4352 tokens.
All inputs are finite; a program needn't handle non-finite values.
Results may differ from the reference program's by a relative error of at most 0.012.
Values may be sent and summed in bfloat16 or wider, within the bound.
No kernel may reach another device: no remote copies, remote signals or barrier semaphores. Data moves between devices by JAX's collectives and lax.ppermute only.
A program may use at most 128 MiB of HBM per device.

```python
import math
import jax
import jax.numpy as jnp
import numpy as np
from jax import lax

D = 2048
HEADS = 16
HEAD_DIM = 128
GROUP = 64
DOCS = 16
TOKENS = 8192
MAX_DOC = 4352


def steps_of(key, dims, pieces, low, top_value):
    gain = 1.0
    for axis_at, blocks in pieces:
        steps = jax.random.uniform(jax.random.fold_in(jax.random.fold_in(key, 6), axis_at), (blocks,), jnp.float32, low / len(pieces), top_value / len(pieces))
        gain = gain * jnp.repeat(jnp.exp(steps), dims[axis_at] // blocks).reshape((-1,) + (1,) * (len(dims) - 1 - axis_at))
    return gain


def length_profile(amount, total, most, slope):
    portions = [(1 << 20) // math.isqrt(standing ** slope) + 1 for standing in range(2, amount + 1)]
    surplus, given = total - most - (amount - 1), [1] * (amount - 1)
    while surplus > 0:
        movable = [i for i in range(amount - 1) if given[i] < most]
        pool, remaining = sum([portions[i] for i in movable]), surplus
        for i in movable:
            addition = min(most - given[i], max(1, remaining * portions[i] // pool), surplus)
            given[i] = given[i] + addition
            surplus = surplus - addition
    return np.array([most] + given)


def ragged(key, number_of, total, reach, skew):
    if number_of == 2:
        one = jax.random.randint(key, (), max(1, total - reach), min(reach, total - 1) + 1)
        return jnp.stack([one, total - one])
    tallies = jnp.asarray(length_profile(number_of, total, reach, skew), jnp.int32)
    twos = (number_of - 1) // 2
    giver, taker = tallies[1:1 + 2 * twos:2], tallies[2:2 + 2 * twos:2]
    margin = jnp.minimum(giver - 1, reach - taker)
    passed = jax.random.randint(jax.random.fold_in(key, 1), (twos,), 0, 1 << 20) % (margin + 1)
    tallies = tallies.at[1:1 + 2 * twos:2].set(giver - passed).at[2:2 + 2 * twos:2].set(taker + passed)
    return tallies[jax.random.permutation(jax.random.fold_in(key, 2), number_of)]


def normal_values(rng, shape, spread, limit, split=(), held_as=jnp.bfloat16):
    values = spread * jax.random.normal(rng, shape, jnp.float32)
    if split:
        values = values * steps_of(rng, shape, split, -0.22, 0.18)
    return jnp.clip(values, -limit, limit).astype(held_as)


def setup_inputs(seed: int = 0) -> dict:
    arg_keys = jax.random.split(jax.random.key(seed), 10)
    tokens = normal_values(arg_keys[0], (TOKENS, D), 1.0, 6.0, ((0, 128),))
    w_query = normal_values(arg_keys[1], (D, D), D ** -0.5, 0.125, ((1, 4),))
    w_key_first = normal_values(arg_keys[2], (D, D), D ** -0.5, 0.125, ((1, 4),))
    w_key_second = normal_values(arg_keys[3], (D, D), D ** -0.5, 0.125, ((1, 4),))
    w_value_first = normal_values(arg_keys[4], (D, D), D ** -0.5, 0.125, ((1, 4),))
    w_value_second = normal_values(arg_keys[5], (D, D), D ** -0.5, 0.125, ((1, 4),))
    w_out = normal_values(arg_keys[6], (D, D), D ** -0.5, 0.125, ((0, 4),))
    lengths = ragged(arg_keys[7], DOCS, TOKENS, MAX_DOC, 2).astype(jnp.int32)
    out_cotangent = normal_values(arg_keys[8], (TOKENS, D), 1.0, 6.0, ((0, 128),))
    return {"tokens": tokens, "w_query": w_query, "w_key_first": w_key_first, "w_key_second": w_key_second, "w_value_first": w_value_first, "w_value_second": w_value_second, "w_out": w_out, "lengths": lengths, "out_cotangent": out_cotangent}


epsilon = 1e-06
precise = lax.Precision.HIGHEST

def start_flags(lengths, positions):
    doc_first = jnp.cumsum(lengths) - lengths
    return jnp.any(positions[:, None] == doc_first[None, :], axis=1).astype(jnp.int32)

def unit_norm(raw_key):
    return raw_key / jnp.sqrt(lax.optimization_barrier(jnp.sum(raw_key * raw_key, axis=-1, keepdims=True)) + epsilon)

def group_step(memory, inputs):
    queries, key_first, key_second, value_first, value_second, starts = inputs
    block_len = queries.shape[0]
    key_rows = jnp.stack([unit_norm(key_first), unit_norm(key_second)], axis=1).reshape(2 * block_len, queries.shape[1], queries.shape[2])
    value_rows = jnp.stack([value_first, value_second], axis=1).reshape(2 * block_len, value_first.shape[1], value_first.shape[2])
    counts = jnp.cumsum(starts)
    counts_ref = jnp.repeat(counts, 2)
    incoming = (counts == 0).astype(jnp.float32)
    incoming_ref = (counts_ref == 0).astype(jnp.float32)
    refl_pos = jnp.arange(2 * block_len)
    token_pos = jnp.arange(block_len)
    same_doc = counts_ref[:, None] == counts_ref[None, :]
    strict_lower = jnp.logical_and(refl_pos[None, :] < refl_pos[:, None], same_doc).astype(jnp.float32)
    key_gram = jnp.einsum('rhd,shd->hrs', key_rows, key_rows, precision=precise)
    system = 2.0 * key_gram * strict_lower[None] + jnp.eye(2 * block_len, dtype=jnp.float32)[None]
    carried = jnp.einsum('rhd,hdw->hrw', key_rows, memory, precision=precise)
    right_side = 2.0 * (jnp.transpose(value_rows, (1, 0, 2)) - incoming_ref[None, :, None] * carried)
    updates = lax.linalg.triangular_solve(system, right_side, left_side=True, lower=True, unit_diagonal=True)
    visible = jnp.logical_and(refl_pos[None, :] <= 2 * token_pos[:, None] + 1, counts[:, None] == counts_ref[None, :]).astype(jnp.float32)
    scores = jnp.einsum('thd,shd->hts', queries, key_rows, precision=precise) * visible[None]
    outputs = jnp.einsum('hts,hsw->thw', scores, updates, precision=precise)
    outputs = outputs + incoming[:, None, None] * jnp.einsum('thd,hdw->thw', queries, memory, precision=precise)
    last_count = counts[block_len - 1]
    tail_mask = (counts_ref == last_count).astype(jnp.float32)
    keep_state = (last_count == 0).astype(jnp.float32)
    new_memory = keep_state * memory + jnp.einsum('rhd,hrw->hdw', key_rows * tail_mask[:, None, None], updates, precision=precise)
    return (new_memory, outputs)

def recurrence(queries, key_first, key_second, value_first, value_second, starts, memory, block_len):
    total_rows = queries.shape[0]
    blocks = total_rows // block_len

    def blockify(array_in):
        return array_in.reshape((blocks, block_len) + array_in.shape[1:])
    stacked = (blockify(queries), blockify(key_first), blockify(key_second), blockify(value_first), blockify(value_second), blockify(starts))
    memory_end, outputs = lax.scan(jax.checkpoint(group_step), memory, stacked)
    return (outputs.reshape((total_rows,) + outputs.shape[2:]), memory_end)

def reference(tokens, w_query, w_key_first, w_key_second, w_value_first, w_value_second, w_out, lengths, out_cotangent):
    weights = (w_query, w_key_first, w_key_second, w_value_first, w_value_second)
    starts = start_flags(lengths, jnp.arange(TOKENS, dtype=jnp.int32))
    projected = tuple((jnp.dot(tokens.astype(jnp.float32), weight.astype(jnp.float32), preferred_element_type=jnp.float32).reshape(TOKENS, HEADS, HEAD_DIM) for weight in weights))
    memory = jnp.zeros((HEADS, HEAD_DIM, HEAD_DIM), jnp.float32)

    def mixer_whole(queries, key_first, key_second, value_first, value_second):
        return recurrence(queries, key_first, key_second, value_first, value_second, starts, memory, GROUP)[0]
    mixed, pullback = jax.vjp(mixer_whole, projected[0], projected[1], projected[2], projected[3], projected[4])
    inv_rms = lax.rsqrt(lax.optimization_barrier(jnp.mean(mixed * mixed, axis=-1, keepdims=True)) + epsilon)
    normal = mixed * inv_rms
    normed = normal.astype(jnp.bfloat16).reshape(TOKENS, D)
    result = jnp.dot(normed.astype(jnp.float32), w_out.astype(jnp.float32), preferred_element_type=jnp.float32).astype(jnp.bfloat16)
    grad_normed = lax.dot_general(out_cotangent.astype(jnp.float32), w_out.astype(jnp.float32), (((1,), (1,)), ((), ())), preferred_element_type=jnp.float32).reshape(TOKENS, HEADS, HEAD_DIM)
    grad_mixed = inv_rms * (grad_normed - normal * lax.optimization_barrier(jnp.mean(grad_normed * normal, axis=-1, keepdims=True)))
    proj_grads = pullback(grad_mixed)
    grad_tokens = jnp.zeros((TOKENS, D), jnp.float32)
    for grad_part, weight in zip(proj_grads, weights):
        rounded = grad_part.reshape(TOKENS, D).astype(jnp.bfloat16)
        grad_tokens = grad_tokens + lax.dot_general(rounded.astype(jnp.float32), weight.astype(jnp.float32), (((1,), (1,)), ((), ())), preferred_element_type=jnp.float32)
    return (result, grad_tokens.astype(jnp.bfloat16))
```

```python
import jax
import jax.numpy as jnp
from jax import lax
from jax.experimental import pallas as pl
from jax.experimental.pallas import tpu as pltpu
from jax.sharding import Mesh
from jax.sharding import PartitionSpec as P

HEAD_DIM = 128
GROUP = 64
REFL = 2 * GROUP
CTX = ("ctx_0", "ctx_1", "ctx_2")
ROW = ("ctx_1", "ctx_2")
CTX_HEAD = ("ctx_0", "ctx_1", "ctx_2", "head")
F32 = jnp.float32
BF16 = jnp.bfloat16
epsilon = 1e-06


def dot1(a, b, ca, cb):
    return lax.dot_general(a, b, (((ca,), (cb,)), ((), ())), preferred_element_type=F32)


def split(x):
    high = x.astype(BF16)
    return high, (x - high.astype(F32)).astype(BF16)


def mm(a, b, ca=1, cb=0):
    ah, al = split(a)
    bh, bl = split(b)
    return dot1(ah, bh, ca, cb) + (dot1(ah, bl, ca, cb) + dot1(al, bh, ca, cb))


def iota2(rows, cols, dim):
    return lax.broadcasted_iota(jnp.int32, (rows, cols), dim)


def refl_pos(index):
    return 2 * (index % GROUP) + index // GROUP


def unit_scale(raw):
    return 1.0 / jnp.sqrt(jnp.sum(raw * raw, axis=-1, keepdims=True) + epsilon)


class Masks:
    def __init__(self, rows_ref, cols_ref, groups):
        self.pr = refl_pos(iota2(REFL, REFL, 0))
        self.pc = refl_pos(iota2(REFL, REFL, 1))
        self.eye = (self.pr == self.pc).astype(F32)
        self.before = self.pc < self.pr
        tok = iota2(GROUP, REFL, 0)
        self.reach = (iota2(GROUP, REFL, 1) % GROUP) <= tok
        self.rows = rows_ref[...]
        self.cols = cols_ref[...]
        self.groups = groups

    def of(self, g):
        dc = self.cols[g * REFL : (g + 1) * REFL, :]
        dr = self.rows[g : g + 1, :]
        prev = self.rows[self.groups + g : self.groups + g + 1, :]
        last = self.rows[2 * self.groups + g : 2 * self.groups + g + 1, :]
        strict = jnp.logical_and(self.before, dc == dr)
        visible = jnp.logical_and(self.reach, dc[:GROUP] == dr)
        incoming = (dc == prev).astype(F32)
        tail = (dc == last).astype(F32)
        keep = (last == prev).astype(F32)
        return strict, visible, incoming, tail, keep

    def level(self, s):
        same = (self.pr // (2 * s)) == (self.pc // (2 * s))
        return jnp.logical_and(
            same, jnp.logical_and((self.pr // s) % 2 == 1, (self.pc // s) % 2 == 0)
        )


def group_rows(x, g):
    return x[g * GROUP : (g + 1) * GROUP, :]


def transform_kernel(
    tok_ref, wq_ref, wk1_ref, wk2_ref, wv1_ref, wv2_ref, rows_ref, cols_ref,
    q_ref, k1_ref, k2_ref, t_ref, x_ref, s_ref, qt_ref, ol_ref, y_ref, send_ref,
):
    tok = tok_ref[...]
    groups = tok.shape[0] // GROUP
    q = dot1(tok, wq_ref[...], 1, 0)
    k1 = dot1(tok, wk1_ref[...], 1, 0)
    k2 = dot1(tok, wk2_ref[...], 1, 0)
    v1 = dot1(tok, wv1_ref[...], 1, 0)
    v2 = dot1(tok, wv2_ref[...], 1, 0)
    q_ref[...] = q
    k1_ref[...] = k1
    k2_ref[...] = k2
    u1 = k1 * unit_scale(k1)
    u2 = k2 * unit_scale(k2)
    masks = Masks(rows_ref, cols_ref, groups)
    every = range(groups)
    per = [masks.of(g) for g in every]
    keys = [jnp.concatenate([group_rows(u1, g), group_rows(u2, g)], axis=0) for g in every]
    vals = [jnp.concatenate([group_rows(v1, g), group_rows(v2, g)], axis=0) for g in every]
    lows = [jnp.where(per[g][0], 2.0 * mm(keys[g], keys[g], 1, 1), 0.0) for g in every]
    first = masks.level(1)
    inv = [masks.eye - jnp.where(first, lows[g], 0.0) for g in every]
    s = 2
    while s < REFL:
        at = masks.level(s)
        half = [mm(inv[g], jnp.where(at, lows[g], 0.0)) for g in every]
        inv = [inv[g] - mm(half[g], inv[g]) for g in every]
        s *= 2
    total = None
    for g in every:
        strict, visible, incoming, tail, keep = per[g]
        right = jnp.concatenate([2.0 * incoming * keys[g], 2.0 * vals[g]], axis=1)
        x = mm(inv[g], right)
        qg = group_rows(q, g)
        scores = jnp.where(visible, mm(qg, keys[g], 1, 1), 0.0)
        sx = mm(scores, x)
        t_ref[0, g] = inv[g]
        x_ref[0, g] = x
        s_ref[0, g] = scores
        qt_ref[g * GROUP : (g + 1) * GROUP, :] = incoming[:GROUP] * qg - sx[:, :HEAD_DIM]
        ol_ref[g * GROUP : (g + 1) * GROUP, :] = sx[:, HEAD_DIM:]
        xk = mm(x, keys[g] * tail, 0, 0)
        plain = (iota2(HEAD_DIM, HEAD_DIM, 0) == iota2(HEAD_DIM, HEAD_DIM, 1)).astype(F32)
        trans = keep * plain - xk[:HEAD_DIM]
        shift = xk[HEAD_DIM:]
        y_ref[0, g] = jnp.concatenate([trans, shift], axis=0)
        if total is None:
            total = jnp.concatenate([trans, shift], axis=0)
        else:
            total = mm(total, trans)
            total = jnp.concatenate([total[:HEAD_DIM], total[HEAD_DIM:] + shift], axis=0)
    parts = send_ref.shape[0]
    cut = HEAD_DIM // parts
    for j in range(parts):
        send_ref[j, :HEAD_DIM, :] = total[:HEAD_DIM]
        send_ref[j, HEAD_DIM:, :] = total[HEAD_DIM + j * cut : HEAD_DIM + (j + 1) * cut]


def state_kernel(
    n0_ref, y_ref, qt_ref, ol_ref, gn_ref, n_ref, normed_ref, do_ref, e_ref, c_ref
):
    groups = y_ref.shape[1]
    state = n0_ref[0]
    ends = []
    for g in range(groups):
        n_ref[0, g] = state
        qt = qt_ref[g * GROUP : (g + 1) * GROUP, :]
        mixed = ol_ref[g * GROUP : (g + 1) * GROUP, :] + mm(qt, state, 1, 1)
        inv_rms = lax.rsqrt(jnp.mean(mixed * mixed, axis=-1, keepdims=True) + epsilon)
        normal = mixed * inv_rms
        normed_ref[g * GROUP : (g + 1) * GROUP, :] = normal.astype(BF16)
        gn = gn_ref[g * GROUP : (g + 1) * GROUP, :]
        do = inv_rms * (gn - normal * jnp.mean(gn * normal, axis=-1, keepdims=True))
        do_ref[g * GROUP : (g + 1) * GROUP, :] = do
        end = mm(do, qt, 0, 0)
        e_ref[0, g] = end
        ends.append(end)
        if g + 1 < groups:
            state = mm(state, y_ref[0, g, :HEAD_DIM]) + y_ref[0, g, HEAD_DIM:]
    back = ends[groups - 1]
    for g in reversed(range(groups - 1)):
        back = mm(back, y_ref[0, g, :HEAD_DIM], 1, 1) + ends[g]
    c_ref[0] = back


def backward_kernel(
    dn_ref, y_ref, e_ref, n_ref, x_ref, s_ref, t_ref, q_ref, k1_ref, k2_ref, do_ref,
    rows_ref, cols_ref, wq_ref, wk1_ref, wk2_ref, wv1_ref, wv2_ref, out_ref, acc_ref,
):
    groups = y_ref.shape[1]
    masks = Masks(rows_ref, cols_ref, groups)
    every = range(groups)
    after = [None] * groups
    grad_state = dn_ref[0]
    for g in reversed(every):
        after[g] = grad_state
        if g:
            grad_state = mm(grad_state, y_ref[0, g, :HEAD_DIM], 1, 1) + e_ref[0, g]
    k1 = k1_ref[...]
    k2 = k2_ref[...]
    r1 = unit_scale(k1)
    r2 = unit_scale(k2)
    u1 = k1 * r1
    u2 = k2 * r2
    parts = ([], [], [], [], [])
    for g in every:
        strict, visible, incoming, tail, keep = masks.of(g)
        keys = jnp.concatenate([group_rows(u1, g), group_rows(u2, g)], axis=0)
        scale = jnp.concatenate([group_rows(r1, g), group_rows(r2, g)], axis=0)
        state = n_ref[0, g]
        do = do_ref[g * GROUP : (g + 1) * GROUP, :]
        qg = q_ref[g * GROUP : (g + 1) * GROUP, :]
        upd = x_ref[0, g, :, HEAD_DIM:] - mm(x_ref[0, g, :, :HEAD_DIM], state, 1, 1)
        d_upd = mm(s_ref[0, g], do, 0, 0) + mm(keys * tail, after[g], 1, 1)
        d_right = mm(t_ref[0, g], d_upd, 0, 0)
        d_scores = jnp.where(visible, mm(do, upd, 1, 1), 0.0)
        d_gram = jnp.where(strict, -2.0 * mm(d_right, upd, 1, 1), 0.0)
        d_keys = (
            mm(d_gram, keys)
            + mm(d_gram, keys, 0, 0)
            + mm(-2.0 * incoming * d_right, state)
            + mm(d_scores, qg, 0, 0)
            + tail * mm(upd, after[g])
        )
        d_q = mm(d_scores, keys) + incoming[:GROUP] * mm(do, state)
        d_raw = scale * (d_keys - keys * jnp.sum(keys * d_keys, axis=-1, keepdims=True))
        d_val = 2.0 * d_right
        for part, piece in zip(
            parts, (d_q, d_raw[:GROUP], d_raw[GROUP:], d_val[:GROUP], d_val[GROUP:])
        ):
            part.append(piece)
    summed = None
    for part, w_ref in zip(parts, (wq_ref, wk1_ref, wk2_ref, wv1_ref, wv2_ref)):
        piece = dot1(jnp.concatenate(part, axis=0).astype(BF16), w_ref[...], 1, 1)
        summed = piece if summed is None else summed + piece
    h = pl.program_id(0)

    @pl.when(h == 0)
    def _():
        acc_ref[...] = summed

    @pl.when(h > 0)
    def _():
        acc_ref[...] += summed

    @pl.when(h == pl.num_programs(0) - 1)
    def _():
        out_ref[...] = acc_ref[...].astype(BF16)


def row_chain_kernel(in_ref, out_ref):
    total = in_ref[0]
    out_ref[0] = total
    for d in range(1, in_ref.shape[0]):
        here = in_ref[d]
        total = mm(total, here[:HEAD_DIM])
        total = jnp.concatenate([total[:HEAD_DIM], total[HEAD_DIM:] + here[HEAD_DIM:]], axis=0)
        out_ref[d] = total


def row_states_kernel(at_ref, planes_ref, prefix_ref, out_ref):
    at = at_ref[0]
    state = jnp.zeros((planes_ref.shape[1] - HEAD_DIM, HEAD_DIM), F32)
    for k in range(planes_ref.shape[0] - 1):
        there = planes_ref[k]
        new = mm(state, there[:HEAD_DIM]) + there[HEAD_DIM:]
        state = jnp.where(k < at, new, state)
    out_ref[0] = state
    for d in range(1, prefix_ref.shape[0]):
        out_ref[d] = mm(state, prefix_ref[d - 1, :HEAD_DIM]) + prefix_ref[d - 1, HEAD_DIM:]


def row_back_kernel(in_ref, c_ref, out_ref):
    count = in_ref.shape[0]
    back = c_ref[count - 1]
    for d in reversed(range(count - 1)):
        back = mm(back, in_ref[d, :HEAD_DIM], 1, 1) + c_ref[d]
    out_ref[...] = back


def row_grads_kernel(at_ref, planes_ref, c_planes_ref, in_ref, c_ref, out_ref):
    at = at_ref[0]
    grad = jnp.zeros(c_planes_ref.shape[1:], F32)
    for k in reversed(range(1, planes_ref.shape[0])):
        new = mm(grad, planes_ref[k, :HEAD_DIM], 1, 1) + c_planes_ref[k]
        grad = jnp.where(k > at, new, grad)
    for d in reversed(range(in_ref.shape[0])):
        out_ref[d] = grad
        if d:
            grad = mm(grad, in_ref[d, :HEAD_DIM], 1, 1) + c_ref[d]


def whole(kernel, out_shape, *args, scalar=False):
    specs = [pl.BlockSpec(memory_space=pltpu.VMEM) for _ in args]
    if scalar:
        specs[0] = pl.BlockSpec(memory_space=pltpu.SMEM)
    return pl.pallas_call(
        kernel,
        out_shape=jax.ShapeDtypeStruct(out_shape, F32),
        in_specs=specs,
        out_specs=pl.BlockSpec(memory_space=pltpu.VMEM),
    )(*args)


def lane_block(rows):
    return pl.BlockSpec((rows, HEAD_DIM), lambda h: (0, h))


def per_head(*dims):
    return pl.BlockSpec((1, *dims), lambda h: (h,) + (0,) * len(dims))


def fixed(*dims):
    return pl.BlockSpec(dims, lambda h: (0,) * len(dims))


def document_marks(lengths, base, rows):
    doc_first = jnp.cumsum(lengths) - lengths
    groups = rows // GROUP

    def doc_of(positions):
        return jnp.sum(positions[..., None] >= doc_first, axis=-1).astype(F32)

    here = doc_of(base + jnp.arange(rows, dtype=jnp.int32)).reshape(groups, GROUP)
    starts = base + GROUP * jnp.arange(groups, dtype=jnp.int32)
    twice = jnp.concatenate([here, here], axis=1)
    prev = jnp.broadcast_to(doc_of(starts - 1)[:, None], (groups, REFL))
    last = jnp.broadcast_to(doc_of(starts + GROUP - 1)[:, None], (groups, REFL))
    rows_mark = jnp.concatenate([twice, prev, last, jnp.zeros_like(last)], axis=0)
    cols_mark = jnp.broadcast_to(twice.reshape(groups * REFL, 1), (groups * REFL, HEAD_DIM))
    return rows_mark, cols_mark


def sum_at_owner(value, axis):
    count = lax.axis_size(axis)
    pieces = value.reshape(count, value.shape[0] // count, value.shape[1])
    arrived = lax.all_to_all(pieces, axis, split_axis=0, concat_axis=0, tiled=True)
    return arrived.astype(F32).sum(axis=0).astype(BF16)


def per_device(
    tokens, w_query, w_key_first, w_key_second, w_value_first, w_value_second, w_out,
    lengths, out_cotangent,
):
    weights = (w_query, w_key_first, w_key_second, w_value_first, w_value_second)
    token_rows = lax.all_gather(tokens, "head", axis=0, tiled=True)
    cotangent_rows = lax.all_gather(out_cotangent, "head", axis=0, tiled=True)
    rows, width = token_rows.shape
    local = w_query.shape[1]
    heads = local // HEAD_DIM
    groups = rows // GROUP
    row_size = lax.axis_size(ROW)
    parts = row_size // heads
    cut = HEAD_DIM // parts
    rows_mark, cols_mark = document_marks(lengths, lax.axis_index(CTX) * rows, rows)
    plane_at = lax.axis_index("ctx_0").astype(jnp.int32).reshape(1)

    def shape(*dims):
        return jax.ShapeDtypeStruct(dims, F32)

    w_specs = [pl.BlockSpec((width, HEAD_DIM), lambda h: (0, h)) for _ in weights]
    params = pltpu.CompilerParams(dimension_semantics=("arbitrary",))
    q, k1, k2, inverse, x, scores, reach, local_out, steps, send = pl.pallas_call(
        transform_kernel,
        grid=(heads,),
        in_specs=[fixed(rows, width), *w_specs, fixed(*rows_mark.shape), fixed(*cols_mark.shape)],
        out_specs=[
            lane_block(rows), lane_block(rows), lane_block(rows),
            per_head(groups, REFL, REFL), per_head(groups, REFL, 2 * HEAD_DIM),
            per_head(groups, GROUP, REFL), lane_block(rows), lane_block(rows),
            per_head(groups, 2 * HEAD_DIM, HEAD_DIM),
            pl.BlockSpec((parts, HEAD_DIM + cut, HEAD_DIM), lambda h: (h, 0, 0)),
        ],
        out_shape=[
            shape(rows, local), shape(rows, local), shape(rows, local),
            shape(heads, groups, REFL, REFL), shape(heads, groups, REFL, 2 * HEAD_DIM),
            shape(heads, groups, GROUP, REFL), shape(rows, local), shape(rows, local),
            shape(heads, groups, 2 * HEAD_DIM, HEAD_DIM),
            shape(row_size, HEAD_DIM + cut, HEAD_DIM),
        ],
        compiler_params=params,
        name="transform",
    )(token_rows, *weights, rows_mark, cols_mark)

    owned = lax.all_to_all(send, ROW, split_axis=0, concat_axis=0, tiled=True)
    prefix = whole(row_chain_kernel, owned.shape, owned)
    planes = lax.all_gather(prefix[row_size - 1], "ctx_0")
    row_states = whole(
        row_states_kernel, (row_size, cut, HEAD_DIM), plane_at, planes, prefix, scalar=True
    )
    start = lax.all_to_all(row_states, ROW, split_axis=0, concat_axis=0, tiled=True)
    start = start.reshape(heads, HEAD_DIM, HEAD_DIM)
    grad_normed = dot1(cotangent_rows, w_out, 1, 1)

    states, normed, grad_mixed, ends, carried = pl.pallas_call(
        state_kernel,
        grid=(heads,),
        in_specs=[
            per_head(HEAD_DIM, HEAD_DIM), per_head(groups, 2 * HEAD_DIM, HEAD_DIM),
            lane_block(rows), lane_block(rows), lane_block(rows),
        ],
        out_specs=[
            per_head(groups, HEAD_DIM, HEAD_DIM), lane_block(rows), lane_block(rows),
            per_head(groups, HEAD_DIM, HEAD_DIM), per_head(HEAD_DIM, HEAD_DIM),
        ],
        out_shape=[
            shape(heads, groups, HEAD_DIM, HEAD_DIM),
            jax.ShapeDtypeStruct((rows, local), BF16), shape(rows, local),
            shape(heads, groups, HEAD_DIM, HEAD_DIM), shape(heads, HEAD_DIM, HEAD_DIM),
        ],
        compiler_params=params,
        name="state",
    )(start, steps, reach, local_out, grad_normed)

    owned_back = lax.all_to_all(
        carried.reshape(row_size, cut, HEAD_DIM), ROW, split_axis=0, concat_axis=0, tiled=True
    )
    plane_back = whole(row_back_kernel, (cut, HEAD_DIM), owned, owned_back)
    back_planes = lax.all_gather(plane_back, "ctx_0")
    row_grads = whole(
        row_grads_kernel, (row_size, cut, HEAD_DIM),
        plane_at, planes, back_planes, owned, owned_back, scalar=True,
    )
    end_grad = lax.all_to_all(row_grads, ROW, split_axis=0, concat_axis=0, tiled=True)
    end_grad = end_grad.reshape(heads, HEAD_DIM, HEAD_DIM)

    result = sum_at_owner(dot1(normed, w_out, 1, 0).astype(BF16), "head")

    summed = pl.pallas_call(
        backward_kernel,
        grid=(heads,),
        in_specs=[
            per_head(HEAD_DIM, HEAD_DIM), per_head(groups, 2 * HEAD_DIM, HEAD_DIM),
            per_head(groups, HEAD_DIM, HEAD_DIM), per_head(groups, HEAD_DIM, HEAD_DIM),
            per_head(groups, REFL, 2 * HEAD_DIM), per_head(groups, GROUP, REFL),
            per_head(groups, REFL, REFL), lane_block(rows), lane_block(rows), lane_block(rows),
            lane_block(rows), fixed(*rows_mark.shape), fixed(*cols_mark.shape), *w_specs,
        ],
        out_specs=fixed(rows, width),
        out_shape=jax.ShapeDtypeStruct((rows, width), BF16),
        scratch_shapes=[pltpu.VMEM((rows, width), F32)],
        compiler_params=params,
        name="backward",
    )(
        end_grad, steps, ends, states, x, scores, inverse, q, k1, k2, grad_mixed,
        rows_mark, cols_mark, *weights,
    )
    return (result, sum_at_owner(summed, "head"))


def solution(mesh):
    finer = Mesh(
        mesh.devices.reshape(4, 4, 2, mesh.shape["head"]), ("ctx_0", "ctx_1", "ctx_2", "head")
    )
    placed = (
        P(CTX_HEAD, None),
        P(None, "head"),
        P(None, "head"),
        P(None, "head"),
        P(None, "head"),
        P(None, "head"),
        P("head", None),
        P(),
        P(CTX_HEAD, None),
    )
    return jax.shard_map(
        per_device,
        mesh=finer,
        in_specs=placed,
        out_specs=(P(CTX_HEAD, None), P(CTX_HEAD, None)),
        check_vma=False,
    )
```

```python
import jax
import jax.numpy as jnp
from jax import lax
from jax.experimental import pallas as pl
from jax.experimental.pallas import tpu as pltpu
from jax.sharding import Mesh
from jax.sharding import PartitionSpec as P

HEAD_DIM = 128
GROUP = 64
REFL = 2 * GROUP
CTX = ("ctx_0", "ctx_1", "ctx_2")
ROW = ("ctx_1", "ctx_2")
CTX_HEAD = ("ctx_0", "ctx_1", "ctx_2", "head")
F32 = jnp.float32
BF16 = jnp.bfloat16
epsilon = 1e-06
HEADS_FIRST = 2
HEADS_STATE = 2
HEADS_BACK = 2
MIB = 1 << 20
LIMIT_FIRST = None
LIMIT_STATE = 57 * MIB
LIMIT_BACK = None
LIMIT_ROW = 6 * MIB


def dot1(a, b, ca, cb):
    return lax.dot_general(a, b, (((ca,), (cb,)), ((), ())), preferred_element_type=F32)


def split(x):
    high = x.astype(BF16)
    return high, (x - high.astype(F32)).astype(BF16)


def mm(a, b, ca=1, cb=0):
    ah, al = split(a)
    bh, bl = split(b)
    if a.shape[ca] % 128:
        return dot1(ah, bh, ca, cb) + (dot1(ah, bl, ca, cb) + dot1(al, bh, ca, cb))
    both = dot1(jnp.concatenate([ah, al], ca), jnp.concatenate([bh, bh], cb), ca, cb)
    return both + dot1(ah, bl, ca, cb)


def iota2(rows, cols, dim):
    return lax.broadcasted_iota(jnp.int32, (rows, cols), dim)


def refl_pos(index):
    return 2 * (index % GROUP) + index // GROUP


def unit_scale(raw):
    return 1.0 / jnp.sqrt(jnp.sum(raw * raw, axis=-1, keepdims=True) + epsilon)


class Masks:
    def __init__(self, rows_ref, cols_ref, groups):
        self.pr = refl_pos(iota2(REFL, REFL, 0))
        self.pc = refl_pos(iota2(REFL, REFL, 1))
        self.eye = (self.pr == self.pc).astype(F32)
        self.before = self.pc < self.pr
        tok = iota2(GROUP, REFL, 0)
        self.reach = (iota2(GROUP, REFL, 1) % GROUP) <= tok
        self.rows = rows_ref[...]
        self.cols = cols_ref[...]
        self.groups = groups

    def of(self, g):
        dc = self.cols[g * REFL : (g + 1) * REFL, :]
        dr = self.rows[g : g + 1, :]
        prev = self.rows[self.groups + g : self.groups + g + 1, :]
        last = self.rows[2 * self.groups + g : 2 * self.groups + g + 1, :]
        strict = jnp.logical_and(self.before, dc == dr)
        visible = jnp.logical_and(self.reach, dc[:GROUP] == dr)
        incoming = (dc == prev).astype(F32)
        tail = (dc == last).astype(F32)
        keep = (last == prev).astype(F32)
        return strict, visible, incoming, tail, keep

    def level(self, s):
        same = (self.pr // (2 * s)) == (self.pc // (2 * s))
        return jnp.logical_and(
            same, jnp.logical_and((self.pr // s) % 2 == 1, (self.pc // s) % 2 == 0)
        )


def group_rows(x, g):
    return x[g * GROUP : (g + 1) * GROUP, :]


def heads_in(ref):
    return range(ref.shape[1] // HEAD_DIM)


def lanes(x, h):
    return x[:, h * HEAD_DIM : (h + 1) * HEAD_DIM]


def transform_kernel(
    at_ref, tok0_ref, tok1_ref, tok2_ref, tok3_ref, wq_ref, wk1_ref, wk2_ref, wv1_ref, wv2_ref,
    rows_ref, cols_ref,
    q_ref, k1_ref, k2_ref, t_ref, x_ref, s_ref, qt_ref, ol_ref, y_ref, send_ref, tok_ref,
):
    at = at_ref[0]

    @pl.when(pl.program_id(0) == 0)
    def _():
        for rel, piece in enumerate((tok0_ref, tok1_ref, tok2_ref, tok3_ref)):
            tok_ref[at ^ rel] = piece[...]

    tok = tok_ref[...].reshape(-1, tok_ref.shape[2])
    groups = tok.shape[0] // GROUP
    q = dot1(tok, wq_ref[...], 1, 0)
    k1 = dot1(tok, wk1_ref[...], 1, 0)
    k2 = dot1(tok, wk2_ref[...], 1, 0)
    v1 = dot1(tok, wv1_ref[...], 1, 0)
    v2 = dot1(tok, wv2_ref[...], 1, 0)
    q_ref[...] = q
    k1_ref[...] = k1
    k2_ref[...] = k2
    masks = Masks(rows_ref, cols_ref, groups)
    per = [masks.of(g) for g in range(groups)]
    plain = (iota2(HEAD_DIM, HEAD_DIM, 0) == iota2(HEAD_DIM, HEAD_DIM, 1)).astype(F32)
    every = [(h, g) for h in heads_in(q_ref) for g in range(groups)]
    unit = [
        (lanes(k1, h) * unit_scale(lanes(k1, h)), lanes(k2, h) * unit_scale(lanes(k2, h)))
        for h in heads_in(q_ref)
    ]
    keys = {
        (h, g): jnp.concatenate([group_rows(unit[h][0], g), group_rows(unit[h][1], g)], axis=0)
        for h, g in every
    }
    lows = {i: jnp.where(per[i[1]][0], 2.0 * mm(keys[i], keys[i], 1, 1), 0.0) for i in every}
    first = masks.level(1)
    inv = {i: masks.eye - jnp.where(first, lows[i], 0.0) for i in every}
    s = 2
    while s < REFL:
        here = masks.level(s)
        half = {i: mm(inv[i], jnp.where(here, lows[i], 0.0)) for i in every}
        inv = {i: inv[i] - mm(half[i], inv[i]) for i in every}
        s *= 2
    trans = {}
    shift = {}
    for i in every:
        h, g = i
        strict, visible, incoming, tail, keep = per[g]
        at_rows = slice(g * GROUP, (g + 1) * GROUP)
        at_lanes = slice(h * HEAD_DIM, (h + 1) * HEAD_DIM)
        vals = jnp.concatenate([lanes(group_rows(v1, g), h), lanes(group_rows(v2, g), h)], axis=0)
        right = jnp.concatenate([2.0 * incoming * keys[i], 2.0 * vals], axis=1)
        x = mm(inv[i], right)
        qg = lanes(group_rows(q, g), h)
        scores = jnp.where(visible, mm(qg, keys[i], 1, 1), 0.0)
        sx = mm(scores, x)
        t_ref[h, g] = inv[i]
        x_ref[h, g] = x
        s_ref[h, g] = scores
        qt_ref[at_rows, at_lanes] = incoming[:GROUP] * qg - sx[:, :HEAD_DIM]
        ol_ref[at_rows, at_lanes] = sx[:, HEAD_DIM:]
        xk = mm(x, keys[i] * tail, 0, 0)
        trans[i] = keep * plain - xk[:HEAD_DIM]
        shift[i] = xk[HEAD_DIM:]
        y_ref[h, g, :HEAD_DIM] = trans[i]
        y_ref[h, g, HEAD_DIM:] = shift[i]
    total = {h: jnp.concatenate([trans[h, 0], shift[h, 0]], axis=0) for h in heads_in(q_ref)}
    for g in range(1, groups):
        for h in heads_in(q_ref):
            new = mm(total[h], trans[h, g])
            total[h] = jnp.concatenate([new[:HEAD_DIM], new[HEAD_DIM:] + shift[h, g]], axis=0)
    parts = send_ref.shape[0] // len(heads_in(q_ref))
    cut = HEAD_DIM // parts
    for h in heads_in(q_ref):
        for j in range(parts):
            send_ref[h * parts + j, :HEAD_DIM, :] = total[h][:HEAD_DIM]
            send_ref[h * parts + j, HEAD_DIM:, :] = total[h][
                HEAD_DIM + j * cut : HEAD_DIM + (j + 1) * cut
            ]


def state_kernel(
    at_ref, n0_ref, y_ref, qt_ref, ol_ref, gn_ref, n_ref, normed_ref, do_ref, e_ref, c_ref
):
    at = at_ref[0]
    groups = y_ref.shape[1]
    heads = heads_in(qt_ref)
    state = {h: n0_ref[h] for h in heads}
    ends = {}
    for g in range(groups):
        at_rows = slice(g * GROUP, (g + 1) * GROUP)
        for h in heads:
            n_ref[h, g] = state[h]
        mixed = {
            h: lanes(ol_ref[at_rows, :], h) + mm(lanes(qt_ref[at_rows, :], h), state[h], 1, 1)
            for h in heads
        }
        if g + 1 < groups:
            state = {
                h: mm(state[h], y_ref[h, g, :HEAD_DIM]) + y_ref[h, g, HEAD_DIM:] for h in heads
            }
        grad_rows = gn_ref[at ^ g]
        for h in heads:
            at_lanes = slice(h * HEAD_DIM, (h + 1) * HEAD_DIM)
            inv_rms = lax.rsqrt(jnp.mean(mixed[h] * mixed[h], axis=-1, keepdims=True) + epsilon)
            normal = mixed[h] * inv_rms
            normed_ref[at_rows, at_lanes] = normal.astype(BF16)
            gn = lanes(grad_rows, h)
            do = inv_rms * (gn - normal * jnp.mean(gn * normal, axis=-1, keepdims=True))
            do_ref[at_rows, at_lanes] = do
            ends[h, g] = mm(do, lanes(qt_ref[at_rows, :], h), 0, 0)
            e_ref[h, g] = ends[h, g]
    back = {h: ends[h, groups - 1] for h in heads}
    for g in reversed(range(groups - 1)):
        back = {h: mm(back[h], y_ref[h, g, :HEAD_DIM], 1, 1) + ends[h, g] for h in heads}
    for h in heads:
        c_ref[h] = back[h]


def backward_kernel(
    at_ref, dn_ref, y_ref, e_ref, n_ref, x_ref, s_ref, t_ref, q_ref, k1_ref, k2_ref, do_ref,
    rows_ref, cols_ref, wq_ref, wk1_ref, wk2_ref, wv1_ref, wv2_ref,
    out0_ref, out1_ref, out2_ref, out3_ref, acc_ref,
):
    at = at_ref[0]
    groups = y_ref.shape[1]
    heads = heads_in(q_ref)
    masks = Masks(rows_ref, cols_ref, groups)
    per = [masks.of(g) for g in range(groups)]
    after = {}
    grad_state = {h: dn_ref[h] for h in heads}
    for g in reversed(range(groups)):
        for h in heads:
            after[h, g] = grad_state[h]
        if g:
            grad_state = {
                h: mm(grad_state[h], y_ref[h, g, :HEAD_DIM], 1, 1) + e_ref[h, g] for h in heads
            }
    parts = ([], [], [], [], [])
    for h in heads:
        k1 = lanes(k1_ref[...], h)
        k2 = lanes(k2_ref[...], h)
        r1 = unit_scale(k1)
        r2 = unit_scale(k2)
        u1 = k1 * r1
        u2 = k2 * r2
        mine = ([], [], [], [], [])
        for g in range(groups):
            strict, visible, incoming, tail, keep = per[g]
            at_rows = slice(g * GROUP, (g + 1) * GROUP)
            keys = jnp.concatenate([group_rows(u1, g), group_rows(u2, g)], axis=0)
            scale = jnp.concatenate([group_rows(r1, g), group_rows(r2, g)], axis=0)
            state = n_ref[h, g]
            do = lanes(do_ref[at_rows, :], h)
            qg = lanes(q_ref[at_rows, :], h)
            upd = x_ref[h, g, :, HEAD_DIM:] - mm(x_ref[h, g, :, :HEAD_DIM], state, 1, 1)
            d_upd = mm(s_ref[h, g], do, 0, 0) + mm(keys * tail, after[h, g], 1, 1)
            d_right = mm(t_ref[h, g], d_upd, 0, 0)
            d_scores = jnp.where(visible, mm(do, upd, 1, 1), 0.0)
            d_gram = jnp.where(strict, -2.0 * mm(d_right, upd, 1, 1), 0.0)
            d_keys = (
                mm(d_gram, keys)
                + mm(d_gram, keys, 0, 0)
                + mm(-2.0 * incoming * d_right, state)
                + mm(d_scores, qg, 0, 0)
                + tail * mm(upd, after[h, g])
            )
            d_q = mm(d_scores, keys) + incoming[:GROUP] * mm(do, state)
            d_raw = scale * (d_keys - keys * jnp.sum(keys * d_keys, axis=-1, keepdims=True))
            d_val = 2.0 * d_right
            pieces = (d_q, d_raw[:GROUP], d_raw[GROUP:], d_val[:GROUP], d_val[GROUP:])
            for part, piece in zip(mine, pieces):
                part.append(piece.astype(BF16))
        for part, piece in zip(parts, mine):
            part.append(jnp.concatenate(piece, axis=0))
    summed = None
    for part, w_ref in zip(parts, (wq_ref, wk1_ref, wk2_ref, wv1_ref, wv2_ref)):
        piece = dot1(jnp.concatenate(part, axis=1), w_ref[...], 1, 1)
        summed = piece if summed is None else summed + piece
    summed = summed.reshape(acc_ref.shape)
    step = pl.program_id(0)

    @pl.when(step == 0)
    def _():
        acc_ref[...] = summed

    @pl.when(step > 0)
    def _():
        acc_ref[...] += summed

    @pl.when(step == pl.num_programs(0) - 1)
    def _():
        for rel, out_ref in enumerate((out0_ref, out1_ref, out2_ref, out3_ref)):
            out_ref[...] = acc_ref[at ^ rel].astype(BF16)


def row_chain_kernel(in_ref, out_ref, last_ref):
    total = in_ref[0]
    out_ref[0] = total
    for d in range(1, in_ref.shape[0]):
        here = in_ref[d]
        total = mm(total, here[:HEAD_DIM])
        total = jnp.concatenate([total[:HEAD_DIM], total[HEAD_DIM:] + here[HEAD_DIM:]], axis=0)
        out_ref[d] = total
    last_ref[...] = total


def row_states_kernel(at_ref, p0_ref, p1_ref, p2_ref, p3_ref, prefix_ref, out_ref, planes_ref):
    at = at_ref[1]
    for rel, piece in enumerate((p0_ref, p1_ref, p2_ref, p3_ref)):
        planes_ref[at ^ rel] = piece[...]
    state = jnp.zeros((planes_ref.shape[1] - HEAD_DIM, HEAD_DIM), F32)
    for k in range(planes_ref.shape[0] - 1):
        there = planes_ref[k]
        new = mm(state, there[:HEAD_DIM]) + there[HEAD_DIM:]
        state = jnp.where(k < at, new, state)
    out_ref[0] = state
    for d in range(1, prefix_ref.shape[0]):
        out_ref[d] = mm(state, prefix_ref[d - 1, :HEAD_DIM]) + prefix_ref[d - 1, HEAD_DIM:]


def row_back_kernel(in_ref, c_ref, out_ref):
    count = in_ref.shape[0]
    back = c_ref[count - 1]
    for d in reversed(range(count - 1)):
        back = mm(back, in_ref[d, :HEAD_DIM], 1, 1) + c_ref[d]
    out_ref[...] = back


def row_grads_kernel(
    at_ref, p0_ref, p1_ref, p2_ref, p3_ref, c0_ref, c1_ref, c2_ref, c3_ref, in_ref, c_ref,
    out_ref, planes_ref,
):
    at = at_ref[1]
    for rel, (piece, tail) in enumerate(
        zip((p0_ref, p1_ref, p2_ref, p3_ref), (c0_ref, c1_ref, c2_ref, c3_ref))
    ):
        planes_ref[at ^ rel, :HEAD_DIM] = piece[:HEAD_DIM]
        planes_ref[at ^ rel, HEAD_DIM:] = tail[...]
    grad = jnp.zeros(c0_ref.shape, F32)
    for k in reversed(range(1, planes_ref.shape[0])):
        new = mm(grad, planes_ref[k, :HEAD_DIM], 1, 1) + planes_ref[k, HEAD_DIM:]
        grad = jnp.where(k > at, new, grad)
    for d in reversed(range(in_ref.shape[0])):
        out_ref[d] = grad
        if d:
            grad = mm(grad, in_ref[d, :HEAD_DIM], 1, 1) + c_ref[d]


def whole(kernel, out_shapes, *args, scalar=False, scratch=()):
    specs = [pl.BlockSpec(memory_space=pltpu.VMEM) for _ in args]
    if scalar:
        specs[0] = pl.BlockSpec(memory_space=pltpu.SMEM)
    return pl.pallas_call(
        kernel,
        out_shape=[jax.ShapeDtypeStruct(dims, F32) for dims in out_shapes],
        in_specs=specs,
        out_specs=[pl.BlockSpec(memory_space=pltpu.VMEM) for _ in out_shapes],
        scratch_shapes=[pltpu.VMEM(dims, F32) for dims in scratch],
        compiler_params=pltpu.CompilerParams(vmem_limit_bytes=LIMIT_ROW),
    )(*args)


def exchanged(value, axis):
    count = lax.axis_size(axis)
    return [value] + [
        lax.ppermute(value, axis, [(j, j ^ rel) for j in range(count)]) for rel in range(1, count)
    ]


def lane_block(rows, heads):
    return pl.BlockSpec((rows, heads * HEAD_DIM), lambda h: (0, h))


def per_head(heads, *dims):
    return pl.BlockSpec((heads, *dims), lambda h: (h,) + (0,) * len(dims))


def fixed(*dims):
    return pl.BlockSpec(dims, lambda h: (0,) * len(dims))


def document_marks(lengths, base, rows):
    doc_first = jnp.cumsum(lengths) - lengths
    groups = rows // GROUP

    def doc_of(positions):
        return jnp.sum(positions[..., None] >= doc_first, axis=-1).astype(F32)

    here = doc_of(base + jnp.arange(rows, dtype=jnp.int32)).reshape(groups, GROUP)
    starts = base + GROUP * jnp.arange(groups, dtype=jnp.int32)
    twice = jnp.concatenate([here, here], axis=1)
    prev = jnp.broadcast_to(doc_of(starts - 1)[:, None], (groups, REFL))
    last = jnp.broadcast_to(doc_of(starts + GROUP - 1)[:, None], (groups, REFL))
    rows_mark = jnp.concatenate([twice, prev, last, jnp.zeros_like(last)], axis=0)
    cols_mark = jnp.broadcast_to(twice.reshape(groups * REFL, 1), (groups * REFL, HEAD_DIM))
    return rows_mark, cols_mark


def sum_at_owner(value, axis):
    count = lax.axis_size(axis)
    pieces = value.reshape(count, value.shape[0] // count, value.shape[1])
    arrived = lax.all_to_all(pieces, axis, split_axis=0, concat_axis=0, tiled=True)
    return arrived.astype(F32).sum(axis=0).astype(BF16)


def per_device(
    tokens, w_query, w_key_first, w_key_second, w_value_first, w_value_second, w_out,
    lengths, out_cotangent,
):
    weights = (w_query, w_key_first, w_key_second, w_value_first, w_value_second)
    shards = lax.axis_size("head")
    token_parts = exchanged(tokens, "head")
    cotangent_parts = exchanged(out_cotangent, "head")
    share, width = tokens.shape
    rows = share * shards
    local = w_query.shape[1]
    heads = local // HEAD_DIM
    groups = rows // GROUP
    row_size = lax.axis_size(ROW)
    parts = row_size // heads
    cut = HEAD_DIM // parts
    rows_mark, cols_mark = document_marks(lengths, lax.axis_index(CTX) * rows, rows)
    at = jnp.stack([lax.axis_index("head"), lax.axis_index("ctx_0")]).astype(jnp.int32)
    scalars = pl.BlockSpec(memory_space=pltpu.SMEM)

    def shape(*dims):
        return jax.ShapeDtypeStruct(dims, F32)

    def w_specs(n):
        return [pl.BlockSpec((width, n * HEAD_DIM), lambda h: (0, h)) for _ in weights]

    def params(limit):
        return pltpu.CompilerParams(
            dimension_semantics=("arbitrary",), vmem_limit_bytes=limit
        )

    n = HEADS_FIRST
    q, k1, k2, inverse, x, scores, reach, local_out, steps, send = pl.pallas_call(
        transform_kernel,
        grid=(heads // n,),
        in_specs=[
            scalars, *[fixed(share, width)] * shards, *w_specs(n),
            fixed(*rows_mark.shape), fixed(*cols_mark.shape),
        ],
        out_specs=[
            lane_block(rows, n), lane_block(rows, n), lane_block(rows, n),
            per_head(n, groups, REFL, REFL), per_head(n, groups, REFL, 2 * HEAD_DIM),
            per_head(n, groups, GROUP, REFL), lane_block(rows, n), lane_block(rows, n),
            per_head(n, groups, 2 * HEAD_DIM, HEAD_DIM),
            per_head(n * parts, HEAD_DIM + cut, HEAD_DIM),
        ],
        out_shape=[
            shape(rows, local), shape(rows, local), shape(rows, local),
            shape(heads, groups, REFL, REFL), shape(heads, groups, REFL, 2 * HEAD_DIM),
            shape(heads, groups, GROUP, REFL), shape(rows, local), shape(rows, local),
            shape(heads, groups, 2 * HEAD_DIM, HEAD_DIM),
            shape(row_size, HEAD_DIM + cut, HEAD_DIM),
        ],
        scratch_shapes=[pltpu.VMEM((shards, share, width), BF16)],
        compiler_params=params(LIMIT_FIRST),
        name="transform",
    )(at, *token_parts, *weights, rows_mark, cols_mark)

    owned = lax.all_to_all(send, ROW, split_axis=0, concat_axis=0, tiled=True)
    prefix, plane = whole(row_chain_kernel, [owned.shape, owned.shape[1:]], owned)
    planes = exchanged(plane, "ctx_0")
    plane_scratch = [(len(planes), *plane.shape)]
    (row_states,) = whole(
        row_states_kernel, [(row_size, cut, HEAD_DIM)], at, *planes, prefix,
        scalar=True, scratch=plane_scratch,
    )
    start = lax.all_to_all(row_states, ROW, split_axis=0, concat_axis=0, tiled=True)
    start = start.reshape(heads, HEAD_DIM, HEAD_DIM)
    grad_normed = dot1(jnp.concatenate(cotangent_parts, axis=0), w_out, 1, 1)

    n = HEADS_STATE
    states, normed, grad_mixed, ends, carried = pl.pallas_call(
        state_kernel,
        grid=(heads // n,),
        in_specs=[
            scalars, per_head(n, HEAD_DIM, HEAD_DIM), per_head(n, groups, 2 * HEAD_DIM, HEAD_DIM),
            lane_block(rows, n), lane_block(rows, n),
            pl.BlockSpec((shards, share, n * HEAD_DIM), lambda h: (0, 0, h)),
        ],
        out_specs=[
            per_head(n, groups, HEAD_DIM, HEAD_DIM), lane_block(rows, n), lane_block(rows, n),
            per_head(n, groups, HEAD_DIM, HEAD_DIM), per_head(n, HEAD_DIM, HEAD_DIM),
        ],
        out_shape=[
            shape(heads, groups, HEAD_DIM, HEAD_DIM),
            jax.ShapeDtypeStruct((rows, local), BF16), shape(rows, local),
            shape(heads, groups, HEAD_DIM, HEAD_DIM), shape(heads, HEAD_DIM, HEAD_DIM),
        ],
        compiler_params=params(LIMIT_STATE),
        name="state",
    )(at, start, steps, reach, local_out, grad_normed.reshape(shards, share, local))

    owned_back = lax.all_to_all(
        carried.reshape(row_size, cut, HEAD_DIM), ROW, split_axis=0, concat_axis=0, tiled=True
    )
    (plane_back,) = whole(row_back_kernel, [(cut, HEAD_DIM)], owned, owned_back)
    back_planes = exchanged(plane_back, "ctx_0")
    (row_grads,) = whole(
        row_grads_kernel, [(row_size, cut, HEAD_DIM)],
        at, *planes, *back_planes, owned, owned_back, scalar=True, scratch=plane_scratch,
    )
    end_grad = lax.all_to_all(row_grads, ROW, split_axis=0, concat_axis=0, tiled=True)
    end_grad = end_grad.reshape(heads, HEAD_DIM, HEAD_DIM)

    result = sum_at_owner(dot1(normed, w_out, 1, 0).astype(BF16), "head")

    n = HEADS_BACK
    summed = pl.pallas_call(
        backward_kernel,
        grid=(heads // n,),
        in_specs=[
            scalars, per_head(n, HEAD_DIM, HEAD_DIM), per_head(n, groups, 2 * HEAD_DIM, HEAD_DIM),
            per_head(n, groups, HEAD_DIM, HEAD_DIM), per_head(n, groups, HEAD_DIM, HEAD_DIM),
            per_head(n, groups, REFL, 2 * HEAD_DIM), per_head(n, groups, GROUP, REFL),
            per_head(n, groups, REFL, REFL), lane_block(rows, n), lane_block(rows, n),
            lane_block(rows, n), lane_block(rows, n),
            fixed(*rows_mark.shape), fixed(*cols_mark.shape), *w_specs(n),
        ],
        out_specs=[fixed(share, width)] * shards,
        out_shape=[jax.ShapeDtypeStruct((share, width), BF16)] * shards,
        scratch_shapes=[pltpu.VMEM((shards, share, width), F32)],
        compiler_params=params(LIMIT_BACK),
        name="backward",
    )(
        at, end_grad, steps, ends, states, x, scores, inverse, q, k1, k2, grad_mixed,
        rows_mark, cols_mark, *weights,
    )
    grad_tokens = summed[0].astype(F32)
    for rel in range(1, shards):
        to_owner = [(j, j ^ rel) for j in range(shards)]
        grad_tokens = grad_tokens + lax.ppermute(summed[rel], "head", to_owner).astype(F32)
    return (result, grad_tokens.astype(BF16))


def solution(mesh):
    finer = Mesh(
        mesh.devices.reshape(4, 4, 2, mesh.shape["head"]), ("ctx_0", "ctx_1", "ctx_2", "head")
    )
    placed = (
        P(CTX_HEAD, None),
        P(None, "head"),
        P(None, "head"),
        P(None, "head"),
        P(None, "head"),
        P(None, "head"),
        P("head", None),
        P(),
        P(CTX_HEAD, None),
    )
    return jax.shard_map(
        per_device,
        mesh=finer,
        in_specs=placed,
        out_specs=(P(CTX_HEAD, None), P(CTX_HEAD, None)),
        check_vma=False,
    )
```

```python
import jax
import jax.numpy as jnp
from jax import lax
from jax.experimental import pallas as pl
from jax.experimental.pallas import tpu as pltpu
from jax.sharding import Mesh
from jax.sharding import PartitionSpec as P

HEAD_DIM = 128
GROUP = 64
REFL = 2 * GROUP
CTX = ("ctx_0", "ctx_1", "ctx_2")
ROW = ("ctx_1", "ctx_2")
CTX_HEAD = ("ctx_0", "ctx_1", "ctx_2", "head")
F32 = jnp.float32
BF16 = jnp.bfloat16
epsilon = 1e-06
HEADS_FIRST = 2
HEADS_STATE = 4
HEADS_BACK = 2
MIB = 1 << 20
LIMIT_FIRST = None
LIMIT_STATE = 57 * MIB
LIMIT_BACK = None
LIMIT_ROW = 6 * MIB


def dot1(a, b, ca, cb):
    return lax.dot_general(a, b, (((ca,), (cb,)), ((), ())), preferred_element_type=F32)


def split(x):
    high = x.astype(BF16)
    return high, (x - high.astype(F32)).astype(BF16)


def mm(a, b, ca=1, cb=0):
    return mm_halves(split(a), split(b), ca, cb)


def mm_halves(a, b, ca=1, cb=0):
    ah, al = a
    bh, bl = b
    if ah.shape[ca] % 128:
        return dot1(ah, bh, ca, cb) + (dot1(ah, bl, ca, cb) + dot1(al, bh, ca, cb))
    both = dot1(jnp.concatenate([ah, al], ca), jnp.concatenate([bh, bh], cb), ca, cb)
    return both + dot1(ah, bl, ca, cb)


def iota2(rows, cols, dim):
    return lax.broadcasted_iota(jnp.int32, (rows, cols), dim)


def refl_pos(index):
    return 2 * (index % GROUP) + index // GROUP


def unit_scale(raw):
    return 1.0 / jnp.sqrt(jnp.sum(raw * raw, axis=-1, keepdims=True) + epsilon)


class Masks:
    def __init__(self, rows_ref, groups):
        self.pr = refl_pos(iota2(REFL, REFL, 0))
        self.pc = refl_pos(iota2(REFL, REFL, 1))
        self.eye = (self.pr == self.pc).astype(F32)
        self.before = self.pc < self.pr
        tok = iota2(GROUP, REFL, 0)
        self.reach = (iota2(GROUP, REFL, 1) % GROUP) <= tok
        self.rows = rows_ref[...]
        self.groups = groups

    def of(self, g):
        dr = self.rows[g : g + 1, :]
        dc = jnp.transpose(jnp.broadcast_to(dr, (REFL, REFL)))
        prev = self.rows[self.groups + g : self.groups + g + 1, :]
        last = self.rows[2 * self.groups + g : 2 * self.groups + g + 1, :]
        strict = jnp.logical_and(self.before, dc == dr)
        visible = jnp.logical_and(self.reach, dc[:GROUP] == dr)
        incoming = (dc == prev).astype(F32)
        tail = (dc == last).astype(F32)
        keep = (last == prev).astype(F32)
        return strict, visible, incoming, tail, keep

    def level(self, s):
        same = (self.pr // (2 * s)) == (self.pc // (2 * s))
        return jnp.logical_and(
            same, jnp.logical_and((self.pr // s) % 2 == 1, (self.pc // s) % 2 == 0)
        )


def group_rows(x, g):
    return x[g * GROUP : (g + 1) * GROUP, :]


def heads_in(ref):
    return range(ref.shape[1] // HEAD_DIM)


def lanes(x, h):
    return x[:, h * HEAD_DIM : (h + 1) * HEAD_DIM]


def transform_kernel(
    at_ref, tok0_ref, tok1_ref, tok2_ref, tok3_ref, wq_ref, wk1_ref, wk2_ref, wv1_ref, wv2_ref,
    rows_ref,
    q_ref, k1_ref, k2_ref, t_ref, x_ref, s_ref, qt_ref, ol_ref, y_ref, send_ref, tok_ref,
):
    at = at_ref[0]

    @pl.when(pl.program_id(0) == 0)
    def _():
        for rel, piece in enumerate((tok0_ref, tok1_ref, tok2_ref, tok3_ref)):
            tok_ref[at ^ rel] = piece[...]

    tok = tok_ref[...].reshape(-1, tok_ref.shape[2])
    groups = tok.shape[0] // GROUP
    q = dot1(tok, wq_ref[...], 1, 0)
    k1 = dot1(tok, wk1_ref[...], 1, 0)
    k2 = dot1(tok, wk2_ref[...], 1, 0)
    v1 = dot1(tok, wv1_ref[...], 1, 0)
    v2 = dot1(tok, wv2_ref[...], 1, 0)
    q_ref[...] = q
    k1_ref[...] = k1
    k2_ref[...] = k2
    masks = Masks(rows_ref, groups)
    per = [masks.of(g) for g in range(groups)]
    plain = (iota2(HEAD_DIM, HEAD_DIM, 0) == iota2(HEAD_DIM, HEAD_DIM, 1)).astype(F32)
    every = [(h, g) for h in heads_in(q_ref) for g in range(groups)]
    unit = [
        (lanes(k1, h) * unit_scale(lanes(k1, h)), lanes(k2, h) * unit_scale(lanes(k2, h)))
        for h in heads_in(q_ref)
    ]
    keys = {
        (h, g): jnp.concatenate([group_rows(unit[h][0], g), group_rows(unit[h][1], g)], axis=0)
        for h, g in every
    }
    lows = {i: jnp.where(per[i[1]][0], 2.0 * mm(keys[i], keys[i], 1, 1), 0.0) for i in every}
    first = masks.level(1)
    inv = {i: masks.eye - jnp.where(first, lows[i], 0.0) for i in every}
    s = 2
    while s < REFL:
        here = masks.level(s)
        half = {i: mm(inv[i], jnp.where(here, lows[i], 0.0)) for i in every}
        inv = {i: inv[i] - mm(half[i], inv[i]) for i in every}
        s *= 2
    trans = {}
    shift = {}
    for i in every:
        h, g = i
        strict, visible, incoming, tail, keep = per[g]
        at_rows = slice(g * GROUP, (g + 1) * GROUP)
        at_lanes = slice(h * HEAD_DIM, (h + 1) * HEAD_DIM)
        vals = jnp.concatenate([lanes(group_rows(v1, g), h), lanes(group_rows(v2, g), h)], axis=0)
        right = jnp.concatenate([2.0 * incoming * keys[i], 2.0 * vals], axis=1)
        x = mm(inv[i], right)
        qg = lanes(group_rows(q, g), h)
        scores = jnp.where(visible, mm(qg, keys[i], 1, 1), 0.0)
        sx = mm(scores, x)
        t_ref[h, g] = inv[i]
        x_ref[h, g] = x
        s_ref[h, g] = scores
        qt_ref[at_rows, at_lanes] = incoming[:GROUP] * qg - sx[:, :HEAD_DIM]
        ol_ref[at_rows, at_lanes] = sx[:, HEAD_DIM:]
        xk = mm(x, keys[i] * tail, 0, 0)
        trans[i] = keep * plain - xk[:HEAD_DIM]
        shift[i] = xk[HEAD_DIM:]
        y_ref[h, g, :HEAD_DIM] = trans[i]
        y_ref[h, g, HEAD_DIM:] = shift[i]
    total = {h: jnp.concatenate([trans[h, 0], shift[h, 0]], axis=0) for h in heads_in(q_ref)}
    for g in range(1, groups):
        for h in heads_in(q_ref):
            new = mm(total[h], trans[h, g])
            total[h] = jnp.concatenate([new[:HEAD_DIM], new[HEAD_DIM:] + shift[h, g]], axis=0)
    parts = send_ref.shape[0] // len(heads_in(q_ref))
    cut = HEAD_DIM // parts
    for h in heads_in(q_ref):
        for j in range(parts):
            send_ref[h * parts + j, :HEAD_DIM, :] = total[h][:HEAD_DIM]
            send_ref[h * parts + j, HEAD_DIM:, :] = total[h][
                HEAD_DIM + j * cut : HEAD_DIM + (j + 1) * cut
            ]


def state_kernel(
    at_ref, n0_ref, y_ref, qt_ref, ol_ref, gn_ref, n_ref, normed_ref, do_ref, e_ref, c_ref
):
    at = at_ref[0]
    groups = y_ref.shape[1]
    heads = heads_in(qt_ref)
    state = {h: n0_ref[h] for h in heads}
    ends = {}
    for g in range(groups):
        at_rows = slice(g * GROUP, (g + 1) * GROUP)
        for h in heads:
            n_ref[h, g] = state[h]
        mixed = {
            h: lanes(ol_ref[at_rows, :], h) + mm(lanes(qt_ref[at_rows, :], h), state[h], 1, 1)
            for h in heads
        }
        if g + 1 < groups:
            state = {
                h: mm(state[h], y_ref[h, g, :HEAD_DIM]) + y_ref[h, g, HEAD_DIM:] for h in heads
            }
        grad_rows = gn_ref[at ^ g]
        for h in heads:
            at_lanes = slice(h * HEAD_DIM, (h + 1) * HEAD_DIM)
            inv_rms = lax.rsqrt(jnp.mean(mixed[h] * mixed[h], axis=-1, keepdims=True) + epsilon)
            normal = mixed[h] * inv_rms
            normed_ref[at_rows, at_lanes] = normal.astype(BF16)
            gn = lanes(grad_rows, h)
            do = inv_rms * (gn - normal * jnp.mean(gn * normal, axis=-1, keepdims=True))
            do_ref[at_rows, at_lanes] = do
            ends[h, g] = mm(do, lanes(qt_ref[at_rows, :], h), 0, 0)
            e_ref[h, g] = ends[h, g]
    back = {h: ends[h, groups - 1] for h in heads}
    for g in reversed(range(groups - 1)):
        back = {h: mm(back[h], y_ref[h, g, :HEAD_DIM], 1, 1) + ends[h, g] for h in heads}
    for h in heads:
        c_ref[h] = back[h]


def backward_kernel(
    at_ref, dn_ref, y_ref, e_ref, n_ref, x_ref, s_ref, t_ref, q_ref, k1_ref, k2_ref, do_ref,
    rows_ref, wq_ref, wk1_ref, wk2_ref, wv1_ref, wv2_ref,
    out0_ref, out1_ref, out2_ref, out3_ref, acc_ref,
):
    at = at_ref[0]
    groups = y_ref.shape[1]
    heads = heads_in(q_ref)
    masks = Masks(rows_ref, groups)
    per = [masks.of(g) for g in range(groups)]
    after = {}
    grad_state = {h: dn_ref[h] for h in heads}
    for g in reversed(range(groups)):
        for h in heads:
            after[h, g] = grad_state[h]
        if g:
            grad_state = {
                h: mm(grad_state[h], y_ref[h, g, :HEAD_DIM], 1, 1) + e_ref[h, g] for h in heads
            }
    parts = ([], [], [], [], [])
    for h in heads:
        k1 = lanes(k1_ref[...], h)
        k2 = lanes(k2_ref[...], h)
        r1 = unit_scale(k1)
        r2 = unit_scale(k2)
        u1 = k1 * r1
        u2 = k2 * r2
        mine = ([], [], [], [], [])
        for g in range(groups):
            strict, visible, incoming, tail, keep = per[g]
            at_rows = slice(g * GROUP, (g + 1) * GROUP)
            keys = jnp.concatenate([group_rows(u1, g), group_rows(u2, g)], axis=0)
            scale = jnp.concatenate([group_rows(r1, g), group_rows(r2, g)], axis=0)
            state = n_ref[h, g]
            do = lanes(do_ref[at_rows, :], h)
            qg = lanes(q_ref[at_rows, :], h)
            upd = x_ref[h, g, :, HEAD_DIM:] - mm(x_ref[h, g, :, :HEAD_DIM], state, 1, 1)
            d_upd = mm(s_ref[h, g], do, 0, 0) + mm(keys * tail, after[h, g], 1, 1)
            d_right = mm(t_ref[h, g], d_upd, 0, 0)
            d_scores = jnp.where(visible, mm(do, upd, 1, 1), 0.0)
            d_gram = jnp.where(strict, -2.0 * mm(d_right, upd, 1, 1), 0.0)
            d_keys = (
                mm(d_gram, keys)
                + mm(d_gram, keys, 0, 0)
                + mm(-2.0 * incoming * d_right, state)
                + mm(d_scores, qg, 0, 0)
                + tail * mm(upd, after[h, g])
            )
            d_q = mm(d_scores, keys) + incoming[:GROUP] * mm(do, state)
            d_raw = scale * (d_keys - keys * jnp.sum(keys * d_keys, axis=-1, keepdims=True))
            d_val = 2.0 * d_right
            pieces = (d_q, d_raw[:GROUP], d_raw[GROUP:], d_val[:GROUP], d_val[GROUP:])
            for part, piece in zip(mine, pieces):
                part.append(piece.astype(BF16))
        for part, piece in zip(parts, mine):
            part.append(jnp.concatenate(piece, axis=0))
    summed = None
    for part, w_ref in zip(parts, (wq_ref, wk1_ref, wk2_ref, wv1_ref, wv2_ref)):
        piece = dot1(jnp.concatenate(part, axis=1), w_ref[...], 1, 1)
        summed = piece if summed is None else summed + piece
    summed = summed.reshape(acc_ref.shape)
    step = pl.program_id(0)

    @pl.when(step == 0)
    def _():
        acc_ref[...] = summed

    @pl.when(step > 0)
    def _():
        acc_ref[...] += summed

    @pl.when(step == pl.num_programs(0) - 1)
    def _():
        for rel, out_ref in enumerate((out0_ref, out1_ref, out2_ref, out3_ref)):
            out_ref[...] = acc_ref[at ^ rel].astype(BF16)


def row_chain_kernel(in_ref, out_ref, last_ref):
    total = in_ref[0]
    out_ref[0] = total
    for d in range(1, in_ref.shape[0]):
        here = in_ref[d]
        total = mm(total, here[:HEAD_DIM])
        total = jnp.concatenate([total[:HEAD_DIM], total[HEAD_DIM:] + here[HEAD_DIM:]], axis=0)
        out_ref[d] = total
    last_ref[...] = total


def row_states_kernel(at_ref, p0_ref, p1_ref, p2_ref, p3_ref, prefix_ref, out_ref, planes_ref):
    at = at_ref[1]
    for rel, piece in enumerate((p0_ref, p1_ref, p2_ref, p3_ref)):
        planes_ref[at ^ rel] = piece[...]
    state = jnp.zeros((planes_ref.shape[1] - HEAD_DIM, HEAD_DIM), F32)
    for k in range(planes_ref.shape[0] - 1):
        there = planes_ref[k]
        new = mm(state, there[:HEAD_DIM]) + there[HEAD_DIM:]
        state = jnp.where(k < at, new, state)
    out_ref[0] = state
    for d in range(1, prefix_ref.shape[0]):
        out_ref[d] = mm(state, prefix_ref[d - 1, :HEAD_DIM]) + prefix_ref[d - 1, HEAD_DIM:]


def row_back_kernel(in_ref, c_ref, out_ref):
    count = in_ref.shape[0]
    back = c_ref[count - 1]
    for d in reversed(range(count - 1)):
        back = mm(back, in_ref[d, :HEAD_DIM], 1, 1) + c_ref[d]
    out_ref[...] = back


def row_grads_kernel(
    at_ref, p0_ref, p1_ref, p2_ref, p3_ref, c0_ref, c1_ref, c2_ref, c3_ref, in_ref, c_ref,
    out_ref, planes_ref,
):
    at = at_ref[1]
    for rel, (piece, tail) in enumerate(
        zip((p0_ref, p1_ref, p2_ref, p3_ref), (c0_ref, c1_ref, c2_ref, c3_ref))
    ):
        planes_ref[at ^ rel, :HEAD_DIM] = piece[:HEAD_DIM]
        planes_ref[at ^ rel, HEAD_DIM:] = tail[...]
    grad = jnp.zeros(c0_ref.shape, F32)
    for k in reversed(range(1, planes_ref.shape[0])):
        new = mm(grad, planes_ref[k, :HEAD_DIM], 1, 1) + planes_ref[k, HEAD_DIM:]
        grad = jnp.where(k > at, new, grad)
    for d in reversed(range(in_ref.shape[0])):
        out_ref[d] = grad
        if d:
            grad = mm(grad, in_ref[d, :HEAD_DIM], 1, 1) + c_ref[d]


def whole(kernel, out_shapes, *args, scalar=False, scratch=()):
    specs = [pl.BlockSpec(memory_space=pltpu.VMEM) for _ in args]
    if scalar:
        specs[0] = pl.BlockSpec(memory_space=pltpu.SMEM)
    return pl.pallas_call(
        kernel,
        out_shape=[jax.ShapeDtypeStruct(dims, F32) for dims in out_shapes],
        in_specs=specs,
        out_specs=[pl.BlockSpec(memory_space=pltpu.VMEM) for _ in out_shapes],
        scratch_shapes=[pltpu.VMEM(dims, F32) for dims in scratch],
        compiler_params=pltpu.CompilerParams(vmem_limit_bytes=LIMIT_ROW),
    )(*args)


def exchanged(value, axis):
    count = lax.axis_size(axis)
    return [value] + [
        lax.ppermute(value, axis, [(j, j ^ rel) for j in range(count)]) for rel in range(1, count)
    ]


def lane_block(rows, heads):
    return pl.BlockSpec((rows, heads * HEAD_DIM), lambda h: (0, h))


def per_head(heads, *dims):
    return pl.BlockSpec((heads, *dims), lambda h: (h,) + (0,) * len(dims))


def fixed(*dims):
    return pl.BlockSpec(dims, lambda h: (0,) * len(dims))


def document_marks(lengths, base, rows):
    doc_first = jnp.cumsum(lengths) - lengths
    groups = rows // GROUP

    def doc_of(positions):
        return jnp.sum(positions[..., None] >= doc_first, axis=-1).astype(F32)

    here = doc_of(base + jnp.arange(rows, dtype=jnp.int32)).reshape(groups, GROUP)
    starts = base + GROUP * jnp.arange(groups, dtype=jnp.int32)
    twice = jnp.concatenate([here, here], axis=1)
    prev = jnp.broadcast_to(doc_of(starts - 1)[:, None], (groups, REFL))
    last = jnp.broadcast_to(doc_of(starts + GROUP - 1)[:, None], (groups, REFL))
    return jnp.concatenate([twice, prev, last, jnp.zeros_like(last)], axis=0)


def sum_at_owner(value, axis):
    count = lax.axis_size(axis)
    pieces = value.reshape(count, value.shape[0] // count, value.shape[1])
    arrived = lax.all_to_all(pieces, axis, split_axis=0, concat_axis=0, tiled=True)
    return arrived.astype(F32).sum(axis=0).astype(BF16)


def per_device(
    tokens, w_query, w_key_first, w_key_second, w_value_first, w_value_second, w_out,
    lengths, out_cotangent,
):
    weights = (w_query, w_key_first, w_key_second, w_value_first, w_value_second)
    shards = lax.axis_size("head")
    token_parts = exchanged(tokens, "head")
    cotangent_parts = exchanged(out_cotangent, "head")
    share, width = tokens.shape
    rows = share * shards
    local = w_query.shape[1]
    heads = local // HEAD_DIM
    groups = rows // GROUP
    row_size = lax.axis_size(ROW)
    parts = row_size // heads
    cut = HEAD_DIM // parts
    rows_mark = document_marks(lengths, lax.axis_index(CTX) * rows, rows)
    at = jnp.stack([lax.axis_index("head"), lax.axis_index("ctx_0")]).astype(jnp.int32)
    scalars = pl.BlockSpec(memory_space=pltpu.SMEM)

    def shape(*dims):
        return jax.ShapeDtypeStruct(dims, F32)

    def w_specs(n):
        return [pl.BlockSpec((width, n * HEAD_DIM), lambda h: (0, h)) for _ in weights]

    def params(limit):
        return pltpu.CompilerParams(
            dimension_semantics=("arbitrary",), vmem_limit_bytes=limit
        )

    n = HEADS_FIRST
    q, k1, k2, inverse, x, scores, reach, local_out, steps, send = pl.pallas_call(
        transform_kernel,
        grid=(heads // n,),
        in_specs=[
            scalars, *[fixed(share, width)] * shards, *w_specs(n),
            fixed(*rows_mark.shape),
        ],
        out_specs=[
            lane_block(rows, n), lane_block(rows, n), lane_block(rows, n),
            per_head(n, groups, REFL, REFL), per_head(n, groups, REFL, 2 * HEAD_DIM),
            per_head(n, groups, GROUP, REFL), lane_block(rows, n), lane_block(rows, n),
            per_head(n, groups, 2 * HEAD_DIM, HEAD_DIM),
            per_head(n * parts, HEAD_DIM + cut, HEAD_DIM),
        ],
        out_shape=[
            shape(rows, local), shape(rows, local), shape(rows, local),
            shape(heads, groups, REFL, REFL), shape(heads, groups, REFL, 2 * HEAD_DIM),
            shape(heads, groups, GROUP, REFL), shape(rows, local), shape(rows, local),
            shape(heads, groups, 2 * HEAD_DIM, HEAD_DIM),
            shape(row_size, HEAD_DIM + cut, HEAD_DIM),
        ],
        scratch_shapes=[pltpu.VMEM((shards, share, width), BF16)],
        compiler_params=params(LIMIT_FIRST),
        name="transform",
    )(at, *token_parts, *weights, rows_mark)

    owned = lax.all_to_all(send, ROW, split_axis=0, concat_axis=0, tiled=True)
    prefix, plane = whole(row_chain_kernel, [owned.shape, owned.shape[1:]], owned)
    planes = exchanged(plane, "ctx_0")
    plane_scratch = [(len(planes), *plane.shape)]
    (row_states,) = whole(
        row_states_kernel, [(row_size, cut, HEAD_DIM)], at, *planes, prefix,
        scalar=True, scratch=plane_scratch,
    )
    start = lax.all_to_all(row_states, ROW, split_axis=0, concat_axis=0, tiled=True)
    start = start.reshape(heads, HEAD_DIM, HEAD_DIM)
    grad_normed = dot1(jnp.concatenate(cotangent_parts, axis=0), w_out, 1, 1)

    n = min(HEADS_STATE, heads)
    states, normed, grad_mixed, ends, carried = pl.pallas_call(
        state_kernel,
        grid=(heads // n,),
        in_specs=[
            scalars, per_head(n, HEAD_DIM, HEAD_DIM), per_head(n, groups, 2 * HEAD_DIM, HEAD_DIM),
            lane_block(rows, n), lane_block(rows, n),
            pl.BlockSpec((shards, share, n * HEAD_DIM), lambda h: (0, 0, h)),
        ],
        out_specs=[
            per_head(n, groups, HEAD_DIM, HEAD_DIM), lane_block(rows, n), lane_block(rows, n),
            per_head(n, groups, HEAD_DIM, HEAD_DIM), per_head(n, HEAD_DIM, HEAD_DIM),
        ],
        out_shape=[
            shape(heads, groups, HEAD_DIM, HEAD_DIM),
            jax.ShapeDtypeStruct((rows, local), BF16), shape(rows, local),
            shape(heads, groups, HEAD_DIM, HEAD_DIM), shape(heads, HEAD_DIM, HEAD_DIM),
        ],
        compiler_params=params(LIMIT_STATE),
        name="state",
    )(at, start, steps, reach, local_out, grad_normed.reshape(shards, share, local))

    owned_back = lax.all_to_all(
        carried.reshape(row_size, cut, HEAD_DIM), ROW, split_axis=0, concat_axis=0, tiled=True
    )
    (plane_back,) = whole(row_back_kernel, [(cut, HEAD_DIM)], owned, owned_back)
    back_planes = exchanged(plane_back, "ctx_0")
    result_part = dot1(normed, w_out, 1, 0).astype(BF16)
    back_planes, result_part = lax.optimization_barrier((back_planes, result_part))
    (row_grads,) = whole(
        row_grads_kernel, [(row_size, cut, HEAD_DIM)],
        at, *planes, *back_planes, owned, owned_back, scalar=True, scratch=plane_scratch,
    )
    end_grad = lax.all_to_all(row_grads, ROW, split_axis=0, concat_axis=0, tiled=True)
    end_grad = end_grad.reshape(heads, HEAD_DIM, HEAD_DIM)

    result = sum_at_owner(result_part, "head")

    n = HEADS_BACK
    summed = pl.pallas_call(
        backward_kernel,
        grid=(heads // n,),
        in_specs=[
            scalars, per_head(n, HEAD_DIM, HEAD_DIM), per_head(n, groups, 2 * HEAD_DIM, HEAD_DIM),
            per_head(n, groups, HEAD_DIM, HEAD_DIM), per_head(n, groups, HEAD_DIM, HEAD_DIM),
            per_head(n, groups, REFL, 2 * HEAD_DIM), per_head(n, groups, GROUP, REFL),
            per_head(n, groups, REFL, REFL), lane_block(rows, n), lane_block(rows, n),
            lane_block(rows, n), lane_block(rows, n),
            fixed(*rows_mark.shape), *w_specs(n),
        ],
        out_specs=[fixed(share, width)] * shards,
        out_shape=[jax.ShapeDtypeStruct((share, width), BF16)] * shards,
        scratch_shapes=[pltpu.VMEM((shards, share, width), F32)],
        compiler_params=params(LIMIT_BACK),
        name="backward",
    )(
        at, end_grad, steps, ends, states, x, scores, inverse, q, k1, k2, grad_mixed,
        rows_mark, *weights,
    )
    grad_tokens = summed[0].astype(F32)
    for rel in range(1, shards):
        to_owner = [(j, j ^ rel) for j in range(shards)]
        grad_tokens = grad_tokens + lax.ppermute(summed[rel], "head", to_owner).astype(F32)
    return (result, grad_tokens.astype(BF16))


def solution(mesh):
    finer = Mesh(
        mesh.devices.reshape(4, 4, 2, mesh.shape["head"]), ("ctx_0", "ctx_1", "ctx_2", "head")
    )
    placed = (
        P(CTX_HEAD, None),
        P(None, "head"),
        P(None, "head"),
        P(None, "head"),
        P(None, "head"),
        P(None, "head"),
        P("head", None),
        P(),
        P(CTX_HEAD, None),
    )
    return jax.shard_map(
        per_device,
        mesh=finer,
        in_specs=placed,
        out_specs=(P(CTX_HEAD, None), P(CTX_HEAD, None)),
        check_vma=False,
    )
```
